32 devices in a mesh: seq: 8 (over y, x, core), vid: 4 (over z).
Axes of the slice: x: 2, y: 2, z: 4, core: 2. Of those that a mesh axis runs over, the one named last changes fastest.
Arguments:
- tokens: bfloat16 [32768, 768], P(('vid', 'seq')), parts along dimension 0, may hold values from -100 to 100
- latents: bfloat16 [2048, 768], P(('vid', 'seq')), parts along dimension 0, may hold values from -6 to 6
- read_weights: bfloat16 [4, 768, 768], P(None, 'seq'), may hold values from -1 to 1
- later_weights: bfloat16 [8, 768, 768], P(None, 'seq'), may hold values from -1 to 1
- head_scale: float32 [3, 12], replicated, may hold values from 1 to 40
Outputs:
- tokens_out: bfloat16 [32768, 768], P(('vid', 'seq')), parts along dimension 0
- latents_out: float32 [2048, 768], P(('vid', 'seq')), parts along dimension 0
The draws below stay inside these ranges and needn't reach their ends.
There are 4 independent parts, one for each index of `vid`. The reference program is written for one: setup_inputs(seed, part) draws one part's arguments, and reference() takes and returns one part's arrays. A program takes and returns all parts, laid end to end along the dimension named above; an argument that names none is the same for every part. Nothing has to cross between parts.
All inputs are finite; a program needn't handle non-finite values.
Results may differ from the reference program's by a relative error of at most 0.01.
The reference program's roundings to bfloat16 on the way count: a program that leaves them out, or rounds other values in their place, can miss the bound.
Values may be sent and summed in bfloat16 or wider, within the bound.
A program may use at most 64 MiB of HBM per device.

```python
import math
import jax
import jax.numpy as jnp
from jax import lax

D = 768
HEADS = 12
LATENTS = 512
TOK_DEV = 1024
TOKENS = 8192


def latent_base(key):
    return jnp.clip(jax.random.normal(jax.random.fold_in(key, 11), (LATENTS, D), jnp.float32), -6.0, 6.0)


def draw_latents(key, part):
    return latent_base(key).astype(jnp.bfloat16)


def draw_tokens(key, part):
    slab_count = TOKENS // TOK_DEV
    slab_amp = jnp.exp(jax.random.uniform(jax.random.fold_in(key, 3), (slab_count, 1), jnp.float32, math.log(0.3), math.log(3.0)))
    centre = jax.random.normal(jax.random.fold_in(key, 4), (slab_count, D), jnp.float32) * slab_amp
    noise_rows = jax.random.normal(jax.random.fold_in(key, 5), (slab_count, TOK_DEV, D), jnp.float32)
    values = noise_rows + centre[:, None, :]
    return jnp.clip(values.reshape(TOKENS, D), -100.0, 100.0).astype(jnp.bfloat16)


def weight_stack(key, count):
    matrices = jax.random.normal(key, (count, D, D), jnp.float32) / math.sqrt(D)
    return jnp.clip(matrices, -6.0 / math.sqrt(D), 6.0 / math.sqrt(D))


def draw_read_weights(key, part):
    matrices = weight_stack(jax.random.fold_in(key, 21), 4)
    return matrices.astype(jnp.bfloat16)


def draw_later_weights(key, part):
    matrices = weight_stack(jax.random.fold_in(key, 22), 8)
    return matrices.astype(jnp.bfloat16)


def draw_head_scale(key, part):
    values = jnp.exp(jax.random.uniform(jax.random.fold_in(key, 31), (3, HEADS), jnp.float32, 0.0, math.log(4.0)))
    return values


def setup_inputs(seed: int = 0, part: int = 0) -> dict:
    seeds = jax.random.split(jax.random.key(seed), 6)
    own_keys = jax.random.split(jax.random.fold_in(seeds[5], part), 6)
    tokens = draw_tokens(jax.random.fold_in(jax.random.fold_in(seeds[5], part), 71), part)
    latents = draw_latents(jax.random.fold_in(jax.random.fold_in(seeds[5], part), 71), part)
    read_weights = draw_read_weights(jax.random.fold_in(seeds[5], 71), part)
    later_weights = draw_later_weights(jax.random.fold_in(seeds[5], 71), part)
    head_scale = draw_head_scale(jax.random.fold_in(seeds[5], 71), part)
    return {"tokens": tokens, "latents": latents, "read_weights": read_weights, "later_weights": later_weights, "head_scale": head_scale}


epsilon = 1e-06

def norm_rows(values):
    values = values.astype(jnp.float32)
    return values * lax.rsqrt(lax.optimization_barrier(jnp.mean(values * values, axis=-1, keepdims=True)) + epsilon)

def head_norm(values, n_heads):
    by_head = values.reshape(values.shape[0], n_heads, values.shape[1] // n_heads)
    by_head = by_head * lax.rsqrt(lax.optimization_barrier(jnp.mean(by_head * by_head, axis=-1, keepdims=True)) + epsilon)
    return by_head.reshape(values.shape).astype(jnp.bfloat16)

def project(inputs, weight):
    return jnp.dot(inputs, weight, preferred_element_type=jnp.float32)

def head_cols(values, head_index, head_dim):
    return lax.dynamic_slice_in_dim(values, head_index * head_dim, head_dim, 1)

def inner(left, right):
    return lax.dot_general(left, right, (((1,), (1,)), ((), ())), preferred_element_type=jnp.float32)

def attend(queries, key_rows, val_rows, factors, n_heads):
    head_dim = queries.shape[1] // n_heads

    def one_head(packed):
        head_index, factor = packed
        scores = inner(head_cols(queries, head_index, head_dim), head_cols(key_rows, head_index, head_dim)) * (factor / math.sqrt(head_dim))
        row_top = lax.optimization_barrier(jnp.max(scores, axis=1, keepdims=True))
        exp_scores = jnp.exp(scores - row_top)
        weights = (exp_scores / lax.optimization_barrier(jnp.sum(exp_scores, axis=1, keepdims=True))).astype(jnp.bfloat16)
        return jnp.dot(weights, head_cols(val_rows, head_index, head_dim), preferred_element_type=jnp.float32)
    results = lax.map(one_head, (jnp.arange(n_heads, dtype=jnp.int32), factors))
    return results.transpose(1, 0, 2).reshape(queries.shape).astype(jnp.bfloat16)

def read_parts(queries, key_rows, val_rows, factors, n_heads):
    head_dim = queries.shape[1] // n_heads

    def one_head(packed):
        head_index, factor = packed
        scores = inner(head_cols(queries, head_index, head_dim), head_cols(key_rows, head_index, head_dim)) * (factor / math.sqrt(head_dim))
        row_top = lax.optimization_barrier(jnp.max(scores, axis=1))
        exp_scores = jnp.exp(scores - row_top[:, None])
        totals = lax.optimization_barrier(jnp.sum(exp_scores, axis=1))
        summed = jnp.dot(exp_scores.astype(jnp.bfloat16), head_cols(val_rows, head_index, head_dim), preferred_element_type=jnp.float32)
        return (summed.astype(jnp.bfloat16), row_top, totals)
    return lax.map(one_head, (jnp.arange(n_heads, dtype=jnp.int32), factors))

def reference(tokens, latents, read_weights, later_weights, head_scale):
    tok_normed = norm_rows(tokens).astype(jnp.bfloat16)
    read_q = head_norm(project(norm_rows(latents).astype(jnp.bfloat16), read_weights[0]), HEADS)
    read_k = head_norm(project(tok_normed, read_weights[1]), HEADS)
    read_v = project(tok_normed, read_weights[2]).astype(jnp.bfloat16)
    slab_count = TOKENS // TOK_DEV
    key_slabs = read_k.reshape(slab_count, TOK_DEV, D)
    val_slabs = read_v.reshape(slab_count, TOK_DEV, D)

    def one_slab(slab_pair):
        return read_parts(read_q, slab_pair[0], slab_pair[1], head_scale[0], HEADS)
    partials, row_tops, totals = lax.map(one_slab, (key_slabs, val_slabs))
    row_best = lax.optimization_barrier(jnp.max(row_tops, axis=0))
    rescale = jnp.exp(row_tops - row_best[None])
    summed = lax.optimization_barrier(jnp.sum(partials.astype(jnp.float32) * rescale[..., None], axis=0))
    weight_sum = lax.optimization_barrier(jnp.sum(totals * rescale, axis=0))
    read_mixed = summed / weight_sum[..., None]
    read_mix = read_mixed.transpose(1, 0, 2).reshape(LATENTS, D).astype(jnp.bfloat16)
    lat_one = latents.astype(jnp.float32) + project(read_mix, read_weights[3])
    self_normed = norm_rows(lat_one).astype(jnp.bfloat16)
    self_q = head_norm(project(self_normed, later_weights[0]), HEADS)
    self_k = head_norm(project(self_normed, later_weights[1]), HEADS)
    self_v = project(self_normed, later_weights[2]).astype(jnp.bfloat16)
    latents_out = lat_one + project(attend(self_q, self_k, self_v, head_scale[1], HEADS), later_weights[3])
    write_in = norm_rows(latents_out).astype(jnp.bfloat16)
    write_q = head_norm(project(tok_normed, later_weights[4]), HEADS)
    write_k = head_norm(project(write_in, later_weights[5]), HEADS)
    write_v = project(write_in, later_weights[6]).astype(jnp.bfloat16)
    tokens_out = (tokens.astype(jnp.float32) + project(attend(write_q, write_k, write_v, head_scale[2], HEADS), later_weights[7])).astype(jnp.bfloat16)
    return (tokens_out, latents_out)
```

```python
import functools
import math

import jax
import jax.numpy as jnp
from jax import lax
from jax.experimental import pallas as pl
from jax.experimental.pallas import tpu as pltpu
from jax.sharding import PartitionSpec as P

HEADS = 12
LANES = 128
epsilon = 1e-06
LOG2E = math.log2(math.e)
BF16 = jnp.bfloat16
F32 = jnp.float32


def rms(values):
    return values * lax.rsqrt(jnp.mean(values * values, axis=-1, keepdims=True) + epsilon)


def dot(left, right):
    return jnp.dot(left, right, preferred_element_type=F32)


def inner(left, right):
    return lax.dot_general(left, right, (((1,), (1,)), ((), ())), preferred_element_type=F32)


def group_matrix(head_dim):
    size = 2 * LANES
    row = lax.broadcasted_iota(jnp.int32, (size, size), 0) // head_dim
    col = lax.broadcasted_iota(jnp.int32, (size, size), 1) // head_dim
    return jnp.where(row == col, 1.0 / head_dim, 0.0).astype(BF16)


def head_norm(values, group):
    size = group.shape[0]
    parts = []
    for start in range(0, values.shape[1], size):
        block = values[:, start : start + size]
        square = block * block
        high = square.astype(BF16)
        low = (square - high.astype(F32)).astype(BF16)
        mean = dot(high, group) + dot(low, group)
        parts.append((block * lax.rsqrt(mean + epsilon)).astype(BF16))
    return jnp.concatenate(parts, axis=1)


def by_rows(rows, chunk, body):
    chunk = min(chunk, rows)

    def step(index, carry):
        body(pl.ds(pl.multiple_of(index * chunk, chunk), chunk))
        return carry

    lax.fori_loop(0, rows // chunk, step, 0)


def half_masks(head_dim):
    lane = lax.broadcasted_iota(jnp.int32, (1, LANES), 1) // head_dim
    return [(lane == part).astype(F32).astype(BF16) for part in range(LANES // head_dim)]


def merge_halves(parts, head_dim):
    lane = lax.broadcasted_iota(jnp.int32, parts[0].shape, 1) // head_dim
    result = parts[0]
    for part in range(1, len(parts)):
        result = jnp.where(lane == part, parts[part], result)
    return result


def attention(q_ref, k_ref, v_ref, scale_ref, which, out_ref, stats_ref, chunk, hooks=None):
    rows, width = q_ref.shape
    head_dim = width // HEADS
    per_block = LANES // head_dim
    chunk = min(chunk, rows)
    n_chunks = rows // chunk
    masks = half_masks(head_dim)
    root = 1.0 / math.sqrt(head_dim)

    def step(index, carry):
        for when, action in (hooks or {}).items():
            pl.when(index == when)(action)
        block = index // n_chunks
        part = index % n_chunks
        cols = pl.ds(pl.multiple_of(block * LANES, LANES), LANES)
        here = pl.ds(pl.multiple_of(part * chunk, chunk), chunk)
        q = q_ref[here, cols]
        k = k_ref[:, cols]
        v = v_ref[:, cols]
        results = []
        for half in range(per_block):
            head = block * per_block + half
            factor = scale_ref[which, head] * root
            scores = inner(q * masks[half], k)
            top = jnp.max(scores, axis=1, keepdims=True)
            exp_scores = jnp.exp2((scores - top) * (factor * LOG2E))
            total = jnp.sum(exp_scores, axis=1, keepdims=True)
            weights = exp_scores.astype(BF16)
            if stats_ref is not None:
                lane = lax.broadcasted_iota(jnp.int32, (chunk, LANES), 1)
                old = stats_ref[here, :]
                old = jnp.where(lane == head, top * factor, old)
                stats_ref[here, :] = jnp.where(lane == head + LANES // 2, total, old)
            mixed = dot(weights, v)
            results.append(mixed / total if stats_ref is None else mixed)
        out_ref[here, cols] = merge_halves(results, head_dim).astype(BF16)
        return carry

    lax.fori_loop(0, (width // LANES) * n_chunks, step, 0)


def read_body(tok_ref, lat_ref, w_ref, scale_ref, parts_ref, stats_ref, q_ref, k_ref, v_ref):
    group = group_matrix(tok_ref.shape[1] // HEADS)

    stats_ref[...] = jnp.zeros(stats_ref.shape, F32)

    def latent_rows(here):
        normed = rms(lat_ref[here, :].astype(F32)).astype(BF16)
        q_ref[here, :] = head_norm(dot(normed, w_ref[0]), group)

    def token_rows(here):
        normed = rms(tok_ref[here, :].astype(F32)).astype(BF16)
        k_ref[here, :] = head_norm(dot(normed, w_ref[1]), group)
        v_ref[here, :] = dot(normed, w_ref[2]).astype(BF16)

    by_rows(lat_ref.shape[0], 256, latent_rows)
    by_rows(tok_ref.shape[0], 256, token_rows)
    attention(q_ref, k_ref, v_ref, scale_ref, 0, parts_ref, stats_ref, 256)


def combine(got, stats, lat_ref, out_w_ref, w_refs, one_ref, q_ref, kv_ref):
    count = len(got)
    rows, width = got[0].shape
    head_dim = width // HEADS
    group = group_matrix(head_dim)
    per_block = LANES // head_dim
    best = functools.reduce(jnp.maximum, stats)
    rescale = [jnp.exp(item - best) for item in stats]
    half = LANES // 2
    bottom = sum(rescale[b][:, :half] * stats[b][:, half:] for b in range(count))
    inverse = 1.0 / bottom
    mixed = []
    for block in range(width // LANES):
        cols = slice(block * LANES, block * LANES + LANES)
        total = jnp.zeros((rows, LANES), F32)
        heads = range(block * per_block, block * per_block + per_block)

        def spread(values):
            return merge_halves(
                [jnp.broadcast_to(values[:, h : h + 1], (rows, LANES)) for h in heads], head_dim
            )

        for b in range(count):
            total += got[b][:, cols].astype(F32) * spread(rescale[b])
        mixed.append((total * spread(inverse)).astype(BF16))
    read_mix = jnp.concatenate(mixed, axis=1)
    lat_one = lat_ref[...].astype(F32) + dot(read_mix, out_w_ref[...])
    one_ref[...] = lat_one
    normed = rms(lat_one).astype(BF16)
    q_ref[...] = head_norm(dot(normed, w_refs[0][...]), group)
    kv_ref[:, :width] = head_norm(dot(normed, w_refs[1][...]), group)
    kv_ref[:, width:] = dot(normed, w_refs[2][...]).astype(BF16)


def combine_body(got_ref, stats_ref, lat_ref, out_w_ref, w_ref, one_ref, q_ref, kv_ref):
    count = got_ref.shape[0]
    combine(
        [got_ref[b] for b in range(count)],
        [stats_ref[b] for b in range(count)],
        lat_ref, out_w_ref, [w_ref.at[i] for i in range(3)], one_ref, q_ref, kv_ref,
    )


def self_body(one_ref, q_ref, kv_ref, w_ref, scale_ref, out_ref, in_ref, mix_ref):
    width = one_ref.shape[1]
    attention(
        q_ref, kv_ref.at[:, :width], kv_ref.at[:, width:], scale_ref, 1, mix_ref, None, 64
    )
    latents_out = one_ref[...] + dot(mix_ref[...], w_ref[...])
    out_ref[...] = latents_out
    in_ref[...] = rms(latents_out).astype(BF16)


def write_body(tok_ref, in_ref, w_ref, scale_ref, out_ref, q_ref, k_ref, v_ref, mix_ref):
    group = group_matrix(tok_ref.shape[1] // HEADS)

    def latent_rows(here):
        k_ref[here, :] = head_norm(dot(in_ref[here, :], w_ref[1]), group)
        v_ref[here, :] = dot(in_ref[here, :], w_ref[2]).astype(BF16)

    def token_rows(here):
        normed = rms(tok_ref[here, :].astype(F32)).astype(BF16)
        q_ref[here, :] = head_norm(dot(normed, w_ref[0]), group)

    def out_rows(here):
        out_ref[here, :] = (
            tok_ref[here, :].astype(F32) + dot(mix_ref[here, :], w_ref[3])
        ).astype(out_ref.dtype)

    by_rows(in_ref.shape[0], 256, latent_rows)
    by_rows(tok_ref.shape[0], 256, token_rows)
    attention(q_ref, k_ref, v_ref, scale_ref, 2, mix_ref, None, 256)
    by_rows(tok_ref.shape[0], 256, out_rows)


VM = pl.BlockSpec(memory_space=pltpu.VMEM)
SM = pl.BlockSpec(memory_space=pltpu.SMEM)


def call(body, in_specs, outs, scratch, *args):
    return pl.pallas_call(
        body,
        out_shape=[jax.ShapeDtypeStruct(shape, dtype) for shape, dtype in outs],
        in_specs=in_specs,
        out_specs=[VM] * len(outs),
        scratch_shapes=[pltpu.VMEM(shape, dtype) for shape, dtype in scratch],
        compiler_params=pltpu.CompilerParams(vmem_limit_bytes=56 * 1024 * 1024),
    )(*args)


def gathered(count, tokens, latents, read_weights, later_weights, head_scale):
    own, width = latents.shape
    rows = own * count
    slab = tokens.shape[0]
    read_full = lax.all_gather(read_weights, "seq", axis=1, tiled=True)
    later_full = lax.all_gather(later_weights, "seq", axis=1, tiled=True)
    lat_all = lax.all_gather(latents, "seq", axis=0, tiled=True)
    parts, stats = call(
        read_body,
        [VM, VM, VM, SM],
        [((rows, width), BF16), ((rows, LANES), F32)],
        [((rows, width), BF16), ((slab, width), BF16), ((slab, width), BF16)],
        tokens, lat_all, read_full[:3], head_scale,
    )
    got_parts = lax.all_to_all(
        parts.reshape(count, own, width), "seq", split_axis=0, concat_axis=0, tiled=True
    )
    got_stats = lax.all_to_all(
        stats.reshape(count, own, LANES), "seq", split_axis=0, concat_axis=0, tiled=True
    )
    lat_one, self_q, self_kv = call(
        combine_body,
        [VM] * 5,
        [((own, width), F32), ((own, width), BF16), ((own, 2 * width), BF16)],
        [],
        got_parts, got_stats, latents, read_full[3], later_full[:3],
    )
    all_kv = lax.all_gather(self_kv, "seq", axis=0, tiled=True)
    latents_out, write_in = call(
        self_body,
        [VM, VM, VM, VM, SM],
        [((own, width), F32), ((own, width), BF16)],
        [((own, width), BF16)],
        lat_one, self_q, all_kv, later_full[3], head_scale,
    )
    write_all = lax.all_gather(write_in, "seq", axis=0, tiled=True)
    (tokens_out,) = call(
        write_body,
        [VM, VM, VM, SM],
        [((slab, width), BF16)],
        [((slab, width), BF16), ((rows, width), BF16), ((rows, width), BF16), ((slab, width), BF16)],
        tokens, write_all, later_full[4:], head_scale,
    )
    return tokens_out, latents_out


MESH = pl.DeviceIdType.MESH


class Net:
    def __init__(self, send, recv):
        self.send, self.recv = send, recv
        self.count = 0
        self.sent = []

    def remote(self, src, dst, target):
        item = self.count
        self.count += 1
        copy = pltpu.make_async_remote_copy(
            src_ref=src, dst_ref=dst, send_sem=self.send.at[item], recv_sem=self.recv.at[item],
            device_id=target, device_id_type=MESH,
        )
        self.sent.append(copy)
        return copy

    def local(self, src, dst):
        item = self.count
        self.count += 1
        return pltpu.make_async_copy(src, dst, self.send.at[item])


def once(method):
    @functools.wraps(method)
    def guarded(self):
        if method.__name__ not in self.done:
            self.done.add(method.__name__)
            method(self)

    return guarded


class Place:
    def __init__(self):
        me = lax.axis_index("seq")
        plane = lax.axis_index("vid")
        self.me, self.core, self.chip = me, me % 2, me // 2
        chip = self.chip
        chip_x = chip + 1 - 2 * (chip % 2)
        chip_y = chip + 2 - 4 * (chip // 2)
        self.chips = (chip_x, chip_y, chip_x + 2 - 4 * (chip // 2))
        self.partner = {"seq": me + 1 - 2 * self.core}
        self.peers = [{"seq": 2 * other + self.core} for other in self.chips]
        self.side = plane % 2
        self.opposite = {"vid": plane + 1 - 2 * self.side}


class Weight:
    def __init__(self, net, spot, buffer, cols, pieces, shard, half, whole=False, lean=None):
        self.done = set()
        own = pl.ds(pl.multiple_of(spot.me * shard, shard), shard)
        self.local, self.near = [], []
        for source, offset, size, start in pieces:
            if whole:
                self.local.append(net.local(source, buffer.at[own]))
                self.near.append(net.remote(source, buffer.at[own], spot.partner))
                continue

            def part(core):
                return source.at[:, pl.ds(pl.multiple_of(core * half + offset, LANES), size)]

            target = buffer.at[own, start : start + size]
            self.local.append(net.local(part(spot.core), target))
            self.near.append(net.remote(part(1 - spot.core), target, spot.partner))
        if whole:
            cols = pl.ds(pl.multiple_of(spot.core * half, LANES), half)
        rows = 2 * shard
        chip_x, chip_y, diagonal = spot.chips
        to_x, to_y, _ = spot.peers

        def send(owner, start, size, target):
            block = buffer.at[pl.ds(pl.multiple_of(owner * rows + start, size), size), cols]
            return net.remote(block, block, target)

        to_x_part, to_y_part = spot.side * shard, (1 - spot.side) * shard
        self.first = [
            send(spot.chip, to_x_part, shard, to_x), send(spot.chip, to_y_part, shard, to_y)
        ]
        self.relay = [
            send(chip_x, to_x_part, shard, to_y) if lean != 1 else None,
            send(chip_y, to_y_part, shard, to_x) if lean != 0 else None,
        ]
        self.swap = [
            send(chip_x, to_x_part, shard, spot.opposite),
            send(chip_y, to_y_part, shard, spot.opposite),
        ]
        self.late = []
        self.kept = [0, 1]
        if lean is not None:
            self.kept = [lean]
            part = (to_x_part, to_y_part)[lean]
            self.late = [send(diagonal, part, shard, spot.opposite)]
        self.forward = []
        if whole:
            self.forward = [send(owner, 0, rows, spot.partner) for owner in spot.chips]

    @once
    def fetch(self):
        for copy in self.local + self.near:
            copy.start()

    @once
    def start(self):
        for copy in self.local:
            copy.wait()
        for copy in self.near:
            copy.wait_recv()
        for copy in self.first:
            copy.start()

    @once
    def spread(self):
        for i in range(2):
            self.first[i].wait_recv()
            if i in self.kept:
                self.relay[i].start()
            self.swap[i].start()

    @once
    def close(self):
        self.spread()
        for i in self.kept if self.late else ():
            self.relay[i].wait_recv()
            self.late[0].start()

    @once
    def settle(self):
        self.close()
        for i in self.kept if not self.late else ():
            self.relay[i].wait_recv()
        for copy in self.swap + self.late:
            copy.wait_recv()
        for copy in self.forward:
            copy.start()

    @once
    def need(self):
        self.settle()
        for copy in self.forward:
            copy.wait_recv()


class Rows:
    def __init__(self, net, spot, source, buffer, rows):
        self.done = set()
        to_x, to_y, _ = spot.peers
        half = rows // 2

        def block(owner, start=0, size=rows):
            return buffer.at[pl.ds(pl.multiple_of(owner * rows + start, half), size)]

        def send(owner, start, size, target):
            return net.remote(block(owner, start, size), block(owner, start, size), target)

        owners = [2 * chip + spot.core for chip in spot.chips]
        self.local = net.local(source, block(spot.me))
        self.first = [net.remote(source, block(spot.me), to) for to in (to_x, to_y, spot.partner)]
        self.relay = [send(owners[0], 0, half, to_y), send(owners[1], half, half, to_x)]
        self.forward = [send(owner, 0, rows, spot.partner) for owner in owners]

    @once
    def start(self):
        for copy in self.first:
            copy.start()
        self.local.start()

    @once
    def spread(self):
        for i in range(2):
            self.first[i].wait_recv()
            self.relay[i].start()
            self.forward[i].start()

    @once
    def close(self):
        for copy in self.relay:
            copy.wait_recv()
        self.forward[2].start()

    @once
    def need(self):
        self.spread()
        self.close()
        self.first[2].wait_recv()
        for copy in self.forward:
            copy.wait_recv()
        self.local.wait()


def unit_norm(values, group, gain=None):
    parts = []
    for start in range(0, values.shape[1], group.shape[0]):
        block = values[:, start : start + group.shape[0]]
        size = block.shape[1]
        mean = dot((block * block).astype(BF16), group[:size, :size])
        scaled = block * lax.rsqrt(mean + epsilon)
        if gain is not None:
            scaled = scaled * gain[:, start : start + size]
        parts.append(scaled.astype(BF16))
    return parts[0] if len(parts) == 1 else jnp.concatenate(parts, axis=1)


def head_gain(scale_ref, which, first, heads, head_dim):
    lane = lax.broadcasted_iota(jnp.int32, (1, heads * head_dim), 1) // head_dim
    gain = jnp.zeros(lane.shape, F32)
    for head in range(heads):
        factor = scale_ref[which, first + head] * (LOG2E / math.sqrt(head_dim))
        gain = jnp.where(lane == head, factor, gain)
    return gain


def low_half(shape):
    return lax.broadcasted_iota(jnp.int32, shape, 1) < LANES // 2


def with_ones(values):
    low = low_half((values.shape[0], LANES))
    parts = []
    for start in range(0, values.shape[1], LANES):
        block = values[:, start : start + LANES]
        parts += [jnp.where(low, block, 1.0).astype(BF16), jnp.where(low, 1.0, block).astype(BF16)]
    return jnp.concatenate(parts, axis=1)


def two_heads(q, k, values, first, second, masks):
    first[...] = inner(q * masks[0], k)
    second[...] = inner(q * masks[1], k)
    tops, sums = [], []
    for scores_ref, value in zip((first, second), values):
        scores = scores_ref[...]
        top = jnp.max(scores, axis=1, keepdims=True)
        tops.append(top)
        sums.append(dot(jnp.exp2(scores - top).astype(BF16), value))
    return tops, sums


def quotient(sums):
    low = low_half(sums[0].shape)
    mixed = jnp.where(low, sums[0], sums[1])
    total = pltpu.roll(jnp.where(low, sums[1], sums[0]), LANES // 2, 1)
    return (mixed / total).astype(BF16)


def whole_body(
    count, tok_ref, lat_ref, rw_ref, lw_ref, scale_ref, out_ref, lat_out_ref,
    norm_ref, kvq_ref, w4_ref, wself_ref, wkv_ref, full_ref, lat_all, q_ref, k_ref, va_ref,
    wide_a, wide_b, tall_a, tall_b, parts_ref, stat_ref, got_ref, got_stat, mix_all, one_ref,
    in_ref, sq_ref, sk_ref, sva_ref, att_ref, wq_ref, wk_ref, wva_ref, mix_ref, power_ref, send, recv,
):
    spot = Place()
    net = Net(send, recv)
    own, width = lat_ref.shape
    slab = tok_ref.shape[0]
    rows = own * count
    shard = rw_ref.shape[1]
    half = width // 2
    head_dim = width // HEADS
    heads = HEADS // 2
    blocks = half // LANES
    chip_rows = 2 * own
    group = group_matrix(head_dim)
    masks = half_masks(head_dim)

    barrier = pltpu.get_barrier_semaphore()
    friends = [spot.partner, spot.opposite] + spot.peers
    for friend in friends:
        pl.semaphore_signal(barrier, inc=1, device_id=friend, device_id_type=MESH)
    pl.semaphore_wait(barrier, len(friends))

    def cols(block):
        return pl.ds(pl.multiple_of(spot.core * half + block * LANES, LANES), LANES)

    def chip_block(chip):
        return pl.ds(pl.multiple_of(chip * chip_rows, chip_rows), chip_rows)

    def weight(buffer, start, size, pieces, whole=False, lean=None):
        cut = slice(start, start + size)
        return Weight(net, spot, buffer, cut, pieces, shard, half, whole, lean)

    read = [rw_ref.at[i] for i in range(4)]
    later = [lw_ref.at[i] for i in range(8)]
    kvq = [
        weight(
            kvq_ref.at[j], 0, 3 * LANES,
            [(read[m], j * LANES, LANES, i * LANES) for i, m in enumerate((1, 2, 0))],
        )
        for j in range(blocks)
    ]
    l4 = weight(w4_ref, 0, half, [(later[4], 0, half, 0)])
    l0, l1, l2 = (
        weight(wself_ref, i * half, half, [(later[i], 0, half, i * half)])
        for i in range(3)
    )
    l5, l6 = (
        weight(wkv_ref, i * half, half, [(later[5 + i], 0, half, i * half)]) for i in range(2)
    )
    r3, l3, l7 = (
        weight(full_ref.at[i], 0, half, [(source, 0, half, 0)], True)
        for i, source in enumerate((read[3], later[3], later[7]))
    )
    lat = Rows(net, spot, lat_ref, lat_all, own)
    order = kvq + [l4, r3, l0, l1, l2, l3, l5, l6, l7]

    def go(spread=(), start=()):
        for index in spread:
            order[index].spread()
        for index in start:
            order[index].start()

    lat.start()
    kvq[0].fetch()
    piece = slab // 4
    token_copies = []
    for i in range(4):
        here = pl.ds(i * piece, piece)
        norm_ref[here, :] = rms(tok_ref[here, :].astype(F32)).astype(BF16)
        copy = net.remote(
            norm_ref.at[here], norm_ref.at[pl.ds(slab + i * piece, piece)], spot.partner
        )
        copy.start()
        token_copies.append(copy)
        if i == 0:
            go(start=[0])
            kvq[1].fetch()
            kvq[2].fetch()
    for item in order:
        item.fetch()
    lat.spread()
    go(start=[1])
    go(spread=[0])
    lat.close()
    go(start=[2])
    go(spread=[1])
    for copy in token_copies:
        copy.wait_recv()

    reduce_copies, gather_copies, forward_copies = [], [], []

    def reduce_start(j):
        copies = []
        for place, (peer, chip) in enumerate(zip(spot.peers, spot.chips)):
            theirs = chip_block(chip)
            copies.append(net.remote(parts_ref.at[j, theirs], got_ref.at[j, place], peer))
            copies.append(net.remote(stat_ref.at[j, :, theirs], got_stat.at[j, place], peer))
        for copy in copies:
            copy.start()
        reduce_copies.append(copies)

    def combine(j):
        for copy in reduce_copies[j]:
            copy.wait_recv()
        mine = chip_block(spot.chip)
        stats = [stat_ref[j, :, mine]] + [got_stat[j, i] for i in range(3)]
        parts = [parts_ref[j, mine]] + [got_ref[j, i] for i in range(3)]
        best = functools.reduce(jnp.maximum, stats)
        rescale = [jnp.exp2(item - best) for item in stats]
        totals = [pltpu.roll(item, item.shape[0] - 2, 0) for item in stats]
        bottom = sum(a * b for a, b in zip(rescale, totals))
        table = [item / bottom for item in rescale]
        table.append(jnp.zeros((LANES - 8 * len(table), chip_rows), F32))
        table = jnp.concatenate(table, axis=0).T
        low = low_half((chip_rows, LANES))
        mixed = jnp.zeros((chip_rows, LANES), F32)
        for i, part in enumerate(parts):
            factor = jnp.where(low, table[:, 8 * i : 8 * i + 1], table[:, 8 * i + 1 : 8 * i + 2])
            mixed += part.astype(F32) * factor
        mix_all[mine, cols(j)] = mixed.astype(BF16)
        block = mix_all.at[mine, cols(j)]
        copies = [net.remote(block, block, to) for to in spot.peers + [spot.partner]]
        for copy in copies:
            copy.start()
        gather_copies.append(copies)

    def forward(j):
        copies = []
        for i, chip in enumerate(spot.chips):
            gather_copies[j][i].wait_recv()
            block = mix_all.at[chip_block(chip), cols(j)]
            copies.append(net.remote(block, block, spot.partner))
            copies[-1].start()
        forward_copies.append(copies)

    def forward_need(j):
        gather_copies[j][3].wait_recv()
        for copy in forward_copies[j]:
            copy.wait_recv()

    read_gain = [
        head_gain(scale_ref, 0, spot.core * heads + 2 * j, 2, head_dim) for j in range(blocks)
    ]
    early = [([2], [3]), ([3], [5]), ([5], [7])]
    after = [([], [4]), ([4], [6]), ([6], [])]
    for j in range(blocks):
        kvq[j].need()

        def key_rows(here):
            both = dot(norm_ref[here, :], kvq_ref[j, :, : 2 * LANES])
            k_ref[here, :] = unit_norm(both[:, :LANES], group)
            va_ref[here, :] = with_ones(both[:, LANES:])

        by_rows(2 * slab, 1024, key_rows)
        if j == 0:
            lat.need()
            in_ref[...] = rms(lat_all[...].astype(F32)).astype(BF16)
        q_ref[...] = unit_norm(dot(in_ref[...], kvq_ref[j, :, 2 * LANES :]), group, read_gain[j])
        if j >= 2:
            forward(j - 2)
        go(*early[j])
        tops, sums = two_heads(
            q_ref[...], k_ref[...], [va_ref[:, :LANES], va_ref[:, LANES:]], wide_a, wide_b, masks
        )
        low = low_half(sums[0].shape)
        parts_ref[j] = jnp.where(low, sums[0], sums[1]).astype(BF16)
        lane = lax.broadcasted_iota(jnp.int32, sums[0].shape, 1)
        stat = jnp.where(lane == 2, pltpu.roll(sums[0], LANES // 2, 1), sums[1])
        stat = jnp.where(lane == 0, tops[0], jnp.where(lane == 1, tops[1], stat))
        stat_ref[j] = stat.T[:8]
        reduce_start(j)
        if j >= 1:
            combine(j - 1)
        go(*after[j])

    write_gain = head_gain(scale_ref, 2, spot.core * heads, heads, head_dim)
    l4.need()

    def write_query_rows(here):
        wq_ref[here, :] = unit_norm(dot(norm_ref[here, :], w4_ref[...]), group, write_gain)

    by_rows(2 * slab, 1024, write_query_rows)
    r3.settle()
    forward(blocks - 2)
    combine(blocks - 1)
    go([7], [8, 9])
    forward(blocks - 1)
    r3.need()
    for j in range(blocks):
        forward_need(j)
    one_ref[...] = lat_all[...].astype(F32) + dot(mix_all[...], full_ref[0])
    in_ref[...] = rms(one_ref[...]).astype(BF16)
    l0.need()
    sq_ref[...] = unit_norm(
        dot(in_ref[...], wself_ref[:, :half]), group,
        head_gain(scale_ref, 1, spot.core * heads, heads, head_dim),
    )
    go([8])
    l1.need()
    sk_ref[...] = unit_norm(dot(in_ref[...], wself_ref[:, half : 2 * half]), group)
    go(start=[10])
    l2.need()
    sva_ref[...] = with_ones(dot(in_ref[...], wself_ref[:, 2 * half :]))

    go([9], [11])
    att_copies = [
        net.remote(att_ref.at[:, cols(j)], att_ref.at[:, cols(j)], spot.partner)
        for j in range(blocks)
    ]

    def span(start, size=LANES):
        return pl.ds(pl.multiple_of(start, LANES), size)

    def self_step(j, carry):
        for when in range(1, blocks):
            pl.when(j == when)(att_copies[when - 1].start)
        pl.when(j == blocks - 1)(l3.settle)
        here = span(j * LANES)
        _, sums = two_heads(
            sq_ref[:, here], sk_ref[:, here],
            [sva_ref[:, span((2 * j + i) * LANES)] for i in range(2)],
            tall_a.at[:rows], tall_b.at[:rows], masks,
        )
        att_ref[:, cols(j)] = quotient(sums)
        return carry

    lax.fori_loop(0, blocks, self_step, 0)
    att_copies[-1].start()
    go([10])
    l3.need()
    for copy in att_copies:
        copy.wait_recv()
    one_ref[...] = one_ref[...] + dot(att_ref[...], full_ref[1])
    lat_out_ref[...] = one_ref[pl.ds(pl.multiple_of(spot.me * own, own), own), :]
    in_ref[...] = rms(one_ref[...]).astype(BF16)
    go([11])
    l5.need()
    wk_ref[...] = unit_norm(dot(in_ref[...], wkv_ref[:, :half]), group)

    mix_copies = [
        net.remote(mix_ref.at[0, :, cols(j)], mix_ref.at[1, :, cols(j)], spot.partner)
        for j in range(blocks)
    ]
    steps = 2 * blocks

    def write_scores(index, head):
        part = index // blocks
        here = span((index % blocks) * LANES)
        queries = wq_ref[pl.ds(pl.multiple_of((1 - part) * slab, slab), slab), here]
        return inner(queries * masks[head], wk_ref[:, here])

    def powers(scores_ref):
        scores = scores_ref[...]
        return jnp.exp2(scores - jnp.max(scores, axis=1, keepdims=True)).astype(BF16)

    def score_step(index, carry):
        tall_b[...] = write_scores(index, 1)
        power_ref[index, 0] = powers(tall_a)
        tall_a[...] = write_scores((index + 1) % steps, 0)
        power_ref[index, 1] = powers(tall_b)
        return carry

    tall_a[...] = write_scores(0, 0)
    lax.fori_loop(0, steps, score_step, 0)
    l6.need()
    wva_ref[...] = with_ones(dot(in_ref[...], wkv_ref[:, half:]))

    for index in range(steps):
        if 1 <= index <= blocks:
            mix_copies[index - 1].start()
        part, j = index // blocks, index % blocks
        sums = [
            dot(power_ref[index, i], wva_ref[:, (2 * j + i) * LANES : (2 * j + i + 1) * LANES])
            for i in range(2)
        ]
        mix_ref[part, :, cols(j)] = quotient(sums)

    l7.need()
    for copy in mix_copies:
        copy.wait_recv()

    def out_rows(here):
        out_ref[here, :] = (
            tok_ref[here, :].astype(F32) + dot(mix_ref[1, here, :], full_ref[2])
        ).astype(out_ref.dtype)

    by_rows(slab, 1024, out_rows)
    for copy in net.sent:
        copy.wait_send()


def cube(count, tokens, latents, read_weights, later_weights, head_scale):
    own, width = latents.shape
    rows = own * count
    slab = tokens.shape[0]
    half = width // 2
    blocks = half // LANES
    vmem = lambda *shape: pltpu.VMEM(shape, BF16)
    full = lambda *shape: pltpu.VMEM(shape, F32)
    return pl.pallas_call(
        functools.partial(whole_body, count),
        out_shape=[
            jax.ShapeDtypeStruct(tokens.shape, BF16),
            jax.ShapeDtypeStruct(latents.shape, F32),
        ],
        in_specs=[VM, VM, pl.BlockSpec(memory_space=pl.ANY), pl.BlockSpec(memory_space=pl.ANY), SM],
        out_specs=[VM, VM],
        scratch_shapes=[
            vmem(2 * slab, width),
            vmem(blocks, width, 3 * LANES),
            vmem(width, half),
            vmem(width, 3 * half),
            vmem(width, 2 * half),
            vmem(3, width, width),
            vmem(rows, width),
            vmem(rows, LANES),
            vmem(2 * slab, LANES),
            vmem(2 * slab, 2 * LANES),
            full(rows, 2 * slab),
            full(rows, 2 * slab),
            full(slab, rows),
            full(slab, rows),
            vmem(blocks, rows, LANES),
            full(blocks, 8, rows),
            vmem(blocks, 3, 2 * own, LANES),
            full(blocks, 3, 8, 2 * own),
            vmem(rows, width),
            full(rows, width),
            vmem(rows, width),
            vmem(rows, half),
            vmem(rows, half),
            vmem(rows, 2 * half),
            vmem(rows, width),
            vmem(2 * slab, half),
            vmem(rows, half),
            vmem(rows, 2 * half),
            vmem(2, slab, width),
            vmem(2 * blocks, 2, slab, rows),
            pltpu.SemaphoreType.DMA((320,)),
            pltpu.SemaphoreType.DMA((320,)),
        ],
        compiler_params=pltpu.CompilerParams(
            vmem_limit_bytes=60 * 1024 * 1024, collective_id=0, has_side_effects=True
        ),
    )(tokens, latents, read_weights, later_weights, head_scale)


def solution(mesh):
    placed = (
        P(("vid", "seq"), None),
        P(("vid", "seq"), None),
        P(None, "seq", None),
        P(None, "seq", None),
        P(),
    )
    count = mesh.shape["seq"]
    form = cube if count == 2**3 and mesh.shape["vid"] % 2 == 0 else gathered
    return jax.shard_map(
        functools.partial(form, count),
        mesh=mesh,
        in_specs=placed,
        out_specs=(P(("vid", "seq"), None), P(("vid", "seq"), None)),
        check_vma=False,
    )
```
